32 devices in a mesh: scene: 4 (over x, core), frame: 8 (over z, y).
Axes of the slice: x: 2, y: 2, z: 4, core: 2. Of those that a mesh axis runs over, the one named last changes fastest.
Arguments:
- features: bfloat16 [8192, 1024], P(('scene', 'frame')), parts along dimension 0, may hold values from -1.5 to 1.5
- norm_gain: float32 [1024], replicated, may hold values from 0.1 to 1.9
- w_qkv: bfloat16 [1024, 3072], replicated, may hold values from -1.3125 to 1.3125
- w_out: bfloat16 [1024, 1024], replicated, may hold values from -0.1875 to 0.1875
- counts: int32 [32], P('scene'), parts along dimension 0, may hold values from 1 to 32, as said below
- query_index: int32 [32, 32], P(('scene', 'frame')), parts along dimension 0, may hold values from 0 to 255
- owner: int32 [32], P('scene'), parts along dimension 0, may hold values from 0 to 7
Outputs:
- mixed: bfloat16 [8192, 1024], P(('scene', 'frame')), parts along dimension 0
- correlation: float32 [32, 8, 32, 256], P(('scene', 'frame')), parts along dimension 0
The draws below stay inside these ranges and needn't reach their ends.
There are 4 independent parts, one for each index of `scene`. The reference program is written for one: setup_inputs(seed, part) draws one part's arguments, and reference() takes and returns one part's arrays. A program takes and returns all parts, laid end to end along the dimension named above; an argument that names none is the same for every part. Nothing has to cross between parts.
Inputs may be any that keep to these rules, and one draw needn't show every extreme that they name: `counts`: every frame has at least one query and some frame has exactly 32.
All inputs are finite; a program needn't handle non-finite values.
Results may differ from the reference program's by a relative error of at most 0.017.
The reference program's roundings to bfloat16 on the way (of `normed`, `pw`, `attended` and `rows`) count: a program that leaves them out, or rounds other values in their place, can miss the bound.
Values may be sent and summed in bfloat16 or wider, within the bound.
A program may use at most 256 MiB of HBM per device.

```python
import math
import jax
import jax.numpy as jnp
import numpy as np
from jax import lax

D = 1024
HEADS = 16
HDIM = 64
TOK_DEV = 256
QMAX = 32
FRAMES = 8
TOKENS = 2048


def draw_counts(key, part):
    first = jax.random.fold_in(key, 11)
    second = jax.random.fold_in(key, 12)
    values = jax.random.randint(first, (FRAMES,), 1, QMAX + 1)
    chosen = jax.random.randint(second, (), 0, FRAMES)
    return jnp.where(jnp.arange(FRAMES) == chosen, QMAX, values).astype(jnp.int32)


def draw_w_qkv(key, part):
    base_key = jax.random.fold_in(key, 21)
    head_key = jax.random.fold_in(key, 22)
    other_key = jax.random.fold_in(key, 23)
    base = jax.random.truncated_normal(base_key, -5.25, 5.25, (D, 3 * D), jnp.float32)
    first_head = jax.random.randint(head_key, (), 0, HEADS)
    second_head = (first_head + 1 + jax.random.randint(other_key, (), 0, HEADS - 1)) % HEADS
    first_factor = 4.5
    second_factor = 6.0
    drawn_factor = 1.6
    head_of = jnp.arange(D) // (D // HEADS)
    factor = jnp.where(head_of == first_head, first_factor, jnp.where(head_of == second_head, second_factor, drawn_factor)).astype(jnp.float32)
    query_cols = base[:, :D] * factor[None, :]
    key_cols = base[:, D:2 * D] * factor[None, :]
    whole = jnp.concatenate([query_cols, key_cols, base[:, 2 * D:]], axis=1) * D ** (-0.5)
    return whole.astype(jnp.bfloat16)


def set_ends(entries, key, low, top_value):
    place = [jax.random.randint(jax.random.fold_in(key, axis), (), 0, length) for axis, length in enumerate(entries.shape)]
    widest = entries.shape.index(max(entries.shape))
    next_to = place[:widest] + [(place[widest] + 1) % entries.shape[widest]] + place[widest + 1:]
    return entries.at[tuple(place)].set(low).at[tuple(next_to)].set(top_value)


def steps_of(stream_key, dims, cuts, low, high):
    factor_of, own = 1.0, jax.random.fold_in(stream_key, 6)
    for dim, blocks in cuts:
        draws = jnp.exp(jax.random.uniform(jax.random.fold_in(own, dim), (blocks,), jnp.float32, low / len(cuts), high / len(cuts)))
        factor_of = factor_of * jnp.repeat(draws, dims[dim] // blocks).reshape([-1 if axis == dim else 1 for axis in range(len(dims))])
    return factor_of


def rank_table(number_of, skew):
    loads = [(1 << 20) // math.isqrt(standing ** skew) + 1 for standing in range(1, number_of + 1)]
    deviation = 1 + sum(loads) // (1 << 30)
    return np.cumsum(np.array([max(1, weight // deviation) for weight in loads]))


def skewed_ids(key, shape, amount, lean):
    table = rank_table(amount, lean)
    pick = jax.random.randint(jax.random.fold_in(key, 1), shape, 0, int(table[amount - 1]))
    rank = jnp.searchsorted(jnp.asarray(table, jnp.int32), pick, side="right")
    return jax.random.permutation(jax.random.fold_in(key, 2), amount)[rank].astype(jnp.int32)


def centred(rng, shape, deviation, bound, pieces=(), dtype=jnp.bfloat16):
    drawn = deviation * jax.random.normal(rng, shape, jnp.float32)
    if pieces:
        drawn = drawn * steps_of(rng, shape, pieces, -0.22, 0.18)
    return jnp.clip(drawn, -bound, bound).astype(dtype)


def setup_inputs(seed: int = 0, part: int = 0) -> dict:
    streams_of = jax.random.split(jax.random.key(seed), 8)
    part_splits = jax.random.split(jax.random.fold_in(streams_of[7], part), 8)
    features = centred(part_splits[0], (TOKENS, D), 0.25, 1.5, ((0, 8),))
    norm_gain = jnp.clip(1.0 + 0.18 * jax.random.normal(streams_of[1], (D,), jnp.float32), 0.1, 1.9)
    w_qkv = draw_w_qkv(jax.random.fold_in(streams_of[7], 71), part)
    w_out = centred(streams_of[3], (D, D), D ** -0.5, 0.1875)
    counts = draw_counts(jax.random.fold_in(jax.random.fold_in(streams_of[7], part), 71), part)
    query_index = set_ends(jax.random.randint(part_splits[5], (FRAMES, QMAX), 0, TOK_DEV), jax.random.fold_in(part_splits[5], 1), 0, TOK_DEV - 1).astype(jnp.int32)
    owner = set_ends(skewed_ids(part_splits[6], (FRAMES,), FRAMES, 2), jax.random.fold_in(part_splits[6], 3), 0, FRAMES - 1).astype(jnp.int32)
    return {"features": features, "norm_gain": norm_gain, "w_qkv": w_qkv, "w_out": w_out, "counts": counts, "query_index": query_index, "owner": owner}


def normalize(x, gain):
    xf = x.astype(jnp.float32)
    mean = lax.optimization_barrier(jnp.mean(xf, axis=-1, keepdims=True))
    var = lax.optimization_barrier(jnp.mean((xf - mean) ** 2, axis=-1, keepdims=True))
    return ((xf - mean) * lax.rsqrt(var + 1e-05) * gain).astype(jnp.bfloat16)

def reference(features, norm_gain, w_qkv, w_out, counts, query_index, owner):
    normed = normalize(features, norm_gain)
    proj = jnp.dot(normed, w_qkv, preferred_element_type=jnp.float32)
    scale = 1.0 / HDIM ** 0.5
    q = (proj[:, :D] * scale).astype(jnp.bfloat16)
    k = proj[:, D:2 * D].astype(jnp.bfloat16).reshape(TOKENS, HEADS, HDIM).astype(jnp.float32)
    v = proj[:, 2 * D:].astype(jnp.bfloat16).reshape(TOKENS, HEADS, HDIM).astype(jnp.float32)
    q_frames = q.reshape(FRAMES, TOK_DEV, HEADS, HDIM)

    def attend(q_block):
        s = jnp.einsum('thd,shd->hts', q_block.astype(jnp.float32), k)
        m = lax.optimization_barrier(jnp.max(s, axis=-1, keepdims=True))
        p = jnp.exp(s - m)
        l = lax.optimization_barrier(jnp.sum(p, axis=-1))
        pw = lax.optimization_barrier(p.astype(jnp.bfloat16)).astype(jnp.float32)
        pv = jnp.einsum('hts,shd->thd', pw, v)
        o = pv / jnp.transpose(l)[:, :, None]
        return o.reshape(TOK_DEV, D).astype(jnp.bfloat16)
    attended = lax.map(attend, q_frames).reshape(TOKENS, D)
    mixed = (features.astype(jnp.float32) + jnp.dot(attended, w_out, preferred_element_type=jnp.float32)).astype(jnp.bfloat16)
    framed = mixed.reshape(FRAMES, TOK_DEV, D)
    rows = framed[jnp.arange(FRAMES)[:, None], query_index]
    valid = jnp.arange(QMAX)[None, :] < counts[:, None]
    rows = jnp.where(valid[:, :, None], rows, jnp.zeros_like(rows))
    corr = jnp.einsum('fqd,gtd->gfqt', rows.astype(jnp.float32), framed.astype(jnp.float32)) / D ** 0.5
    owned = owner[None, :] == jnp.arange(FRAMES)[:, None]
    corr = jnp.where(owned[:, :, None, None], corr, jnp.float32(0.0))
    return (mixed, corr)
```

```python
import functools

import jax
import jax.numpy as jnp
from jax import lax
from jax.experimental import pallas as pl
from jax.experimental.pallas import tpu as pltpu
from jax.sharding import PartitionSpec as P

HEADS = 16
MESH = pl.DeviceIdType.MESH
F32 = jnp.float32
BF16 = jnp.bfloat16
NT = (((1,), (1,)), ((), ()))
GROUP = 4


def kernel(
    n,
    f_ref, gain_ref, wqkv_hbm, wo_hbm, counts_ref, index_ref, owner_ref,
    mixed_ref, corr_ref,
    slots, w, wo, wvt, nrm, qt, kb, vt, acc, top, total, rows,
    wsem, send, recv, rsend, rrecv,
):
    tok, d = f_ref.shape
    hd = d // HEADS
    length = n // 2
    me = lax.axis_index("frame")
    a, b = me // 2, me % 2
    across = a * 2 + (1 - b)
    has_left, has_right = a > 0, a < length - 1

    copies = [
        pltpu.make_async_copy(wqkv_hbm, w, wsem.at[0]),
        pltpu.make_async_copy(wo_hbm, wo, wsem.at[1]),
    ]
    for c in copies:
        c.start()

    barrier = pltpu.get_barrier_semaphore()

    def greet(target):
        pl.semaphore_signal(barrier, inc=1, device_id={"frame": target}, device_id_type=MESH)

    pl.when(has_left)(lambda: greet(me - 2))
    pl.when(has_right)(lambda: greet(me + 2))
    greet(across)
    pl.semaphore_wait(
        barrier, 1 + jnp.where(has_left, 1, 0) + jnp.where(has_right, 1, 0)
    )

    def hop(buf, ssem, rsem, src, way, target, source=None):
        return pltpu.make_async_remote_copy(
            src_ref=buf.at[src] if source is None else source,
            dst_ref=buf.at[src],
            send_sem=ssem.at[src // 2, way],
            recv_sem=rsem.at[src],
            device_id={"frame": target},
            device_id_type=MESH,
        )

    def push(buf, ssem, rsem, src, go_right, go_left, source=None):
        pl.when(go_right)(lambda: hop(buf, ssem, rsem, src, 0, me + 2, source).start())
        pl.when(go_left)(lambda: hop(buf, ssem, rsem, src, 1, me - 2, source).start())
        hop(buf, ssem, rsem, src, 2, across, source).start()

    def landed(buf, ssem, rsem, src):
        hop(buf, ssem, rsem, src, 2, across).wait_recv()

    def relay(buf, ssem, rsem, dist):
        @pl.when(a - dist >= 0)
        def _():
            src = me - 2 * dist
            landed(buf, ssem, rsem, src)
            push(buf, ssem, rsem, src, has_right, False)

        @pl.when(a + dist <= length - 1)
        def _():
            src = me + 2 * dist
            landed(buf, ssem, rsem, src)
            push(buf, ssem, rsem, src, False, has_left)

    def drain(buf, ssem, rsem, source=None):
        hop(buf, ssem, rsem, me, 2, across, source).wait_send()
        pl.when(has_right)(lambda: hop(buf, ssem, rsem, me, 0, me + 2, source).wait_send())
        pl.when(has_left)(lambda: hop(buf, ssem, rsem, me, 1, me - 2, source).wait_send())

        @pl.loop(1, length)
        def _(dist):
            @pl.when(a - dist >= 0)
            def _():
                src = me - 2 * dist
                hop(buf, ssem, rsem, src, 2, across).wait_send()
                pl.when(has_right)(lambda: hop(buf, ssem, rsem, src, 0, me + 2).wait_send())

            @pl.when(a + dist <= length - 1)
            def _():
                src = me + 2 * dist
                hop(buf, ssem, rsem, src, 2, across).wait_send()
                pl.when(has_left)(lambda: hop(buf, ssem, rsem, src, 1, me - 2).wait_send())

    push(slots, send, recv, me, has_right, has_left, f_ref)

    near = jnp.minimum(a, length - 1 - a)

    def place(k):
        dist = jnp.where(k <= 2 * near, (k + 1) // 2, k - near)
        left = jnp.where(k <= 2 * near, k % 2 == 1, a >= length - 1 - a)
        return jnp.where(left, a - dist, a + dist)

    def normalize(load):
        step = 32

        @pl.loop(0, tok // step, unroll=2)
        def _(i):
            at = pl.ds(pl.multiple_of(i * step, step), step)
            x = load(at).astype(F32)
            mean = jnp.mean(x, axis=-1, keepdims=True)
            c = x - mean
            var = jnp.mean(c * c, axis=-1, keepdims=True)
            nrm[at, :] = (c * lax.rsqrt(var + 1e-05) * gain_ref[...]).astype(BF16)

    def attend():
        tile = 256
        for c in range(d // tile):
            kb[:, c * tile : (c + 1) * tile] = jnp.dot(
                nrm[...], w[:, d + c * tile : d + (c + 1) * tile], preferred_element_type=F32
            ).astype(BF16)
        for c in range(d // tile):
            vt[c * tile : (c + 1) * tile, :] = lax.dot_general(
                wvt[c * tile : (c + 1) * tile, :], nrm[...], NT, preferred_element_type=F32
            ).astype(BF16)

        @pl.loop(0, HEADS // GROUP)
        def _(g):
            for j in range(GROUP):
                h = g * GROUP + j
                cols = pl.ds(pl.multiple_of((g * GROUP + j // 2 * 2) * hd, 2 * hd), 2 * hd)
                at = pl.ds(pl.multiple_of(h * hd, hd), hd)
                s = jnp.dot(kb[:, cols], qt[h], preferred_element_type=F32)
                old = top[h]
                new = jnp.maximum(old, jnp.max(s, axis=0, keepdims=True))
                fade = jnp.exp(old - new)
                p = jnp.exp(s - new)
                top[h] = new
                total[h] = total[h] * fade + jnp.sum(p, axis=0, keepdims=True)
                acc[at, :] = acc[at, :] * fade + jnp.dot(
                    vt[at, :], p.astype(BF16), preferred_element_type=F32
                )

    normalize(lambda at: f_ref[at, :])
    copies[0].wait()
    pair = 2 * hd
    upper = lax.broadcasted_iota(jnp.int32, (pair, tok), 0) < hd
    for c in range(HEADS // 2):
        q = jnp.dot(nrm[...], w[:, c * pair : (c + 1) * pair], preferred_element_type=F32)
        q = jnp.transpose(q * (1.0 / hd**0.5))
        qt[2 * c] = jnp.where(upper, q, 0.0).astype(BF16)
        qt[2 * c + 1] = jnp.where(upper, 0.0, q).astype(BF16)
    for c in range(d // 128):
        part = w[:, 2 * d + c * 128 : 2 * d + (c + 1) * 128].astype(F32)
        wvt[c * 128 : (c + 1) * 128, :] = jnp.transpose(part).astype(BF16)
    top[...] = jnp.full(top.shape, -1e30, F32)
    total[...] = jnp.zeros_like(total)
    acc[...] = jnp.zeros_like(acc)

    @pl.loop(0, n)
    def _(t):
        odd = t % 2 == 1
        by_line = jnp.logical_and(odd, t < n - 1)

        @pl.when(by_line)
        def _():
            relay(slots, send, recv, (t + 1) // 2)

        near_k = jnp.where(by_line, (t + 1) // 2, jnp.where(odd, length - 1, t // 2 - 1))
        src = jnp.where(
            t == 0, me, place(jnp.maximum(near_k, 0)) * 2 + jnp.where(by_line, b, 1 - b)
        )

        @pl.when(jnp.logical_and(t > 0, jnp.logical_not(by_line)))
        def _():
            landed(slots, send, recv, src)

        @pl.when(t > 0)
        def _():
            normalize(lambda at: slots[src, at, :])

        attend()

    tile = 256
    per = tile // hd
    for c in range(d // tile):
        o = jnp.concatenate(
            [
                acc[h * hd : (h + 1) * hd, :] / total[h]
                for h in range(c * per, (c + 1) * per)
            ],
            axis=0,
        )
        nrm[:, c * tile : (c + 1) * tile] = jnp.transpose(o).astype(BF16)
    copies[1].wait()
    for c in range(d // tile):
        cols = slice(c * tile, (c + 1) * tile)
        mixed_ref[:, cols] = (
            f_ref[:, cols].astype(F32)
            + jnp.dot(nrm[...], wo[:, cols], preferred_element_type=F32)
        ).astype(BF16)

    q = index_ref.shape[1]
    at = lax.broadcasted_iota(jnp.int32, (tok, q), 0)
    slot = lax.broadcasted_iota(jnp.int32, (tok, q), 1)
    chosen = jnp.logical_and(at == index_ref[...], slot < counts_ref[me])
    chosen = jnp.transpose(jnp.where(chosen, 1.0, 0.0).astype(F32)).astype(BF16)
    rows[me] = jnp.dot(chosen, mixed_ref[...], preferred_element_type=F32).astype(BF16)
    push(rows, rsend, rrecv, me, has_right, has_left)

    @pl.loop(1, length)
    def _(dist):
        relay(rows, rsend, rrecv, dist)

    @pl.loop(0, length)
    def _(k):
        landed(rows, rsend, rrecv, place(k) * 2 + 1 - b)

    scale = 1.0 / d**0.5
    for f0 in range(0, n, 8):
        fn = min(8, n - f0)
        block = rows[f0 : f0 + fn].reshape(fn * q, d)
        got = lax.dot_general(block, mixed_ref[...], NT, preferred_element_type=F32)
        for f in range(fn):
            factor = jnp.where(owner_ref[f0 + f] == me, scale, 0.0).astype(F32)
            corr_ref[0, f0 + f] = got[f * q : (f + 1) * q, :] * factor

    drain(slots, send, recv, f_ref)
    drain(rows, rsend, rrecv)


def solution(mesh):
    n = mesh.shape["frame"]

    def per_device(features, norm_gain, w_qkv, w_out, counts, query_index, owner):
        tok, d = features.shape
        q = query_index.shape[1]
        hd = d // HEADS
        vmem = pl.BlockSpec(memory_space=pltpu.VMEM)
        smem = pl.BlockSpec(memory_space=pltpu.SMEM)
        hbm = pl.BlockSpec(memory_space=pl.ANY)
        dma = pltpu.SemaphoreType.DMA
        return pl.pallas_call(
            functools.partial(kernel, n),
            out_shape=(
                jax.ShapeDtypeStruct((tok, d), BF16),
                jax.ShapeDtypeStruct((1, n, q, tok), F32),
            ),
            in_specs=[vmem, vmem, hbm, hbm, smem, vmem, smem],
            out_specs=(vmem, vmem),
            scratch_shapes=[
                pltpu.VMEM((n, tok, d), BF16),
                pltpu.VMEM((d, 3 * d), BF16),
                pltpu.VMEM((d, d), BF16),
                pltpu.VMEM((d, d), BF16),
                pltpu.VMEM((tok, d), BF16),
                pltpu.VMEM((HEADS, 2 * hd, tok), BF16),
                pltpu.VMEM((tok, d), BF16),
                pltpu.VMEM((d, tok), BF16),
                pltpu.VMEM((d, tok), F32),
                pltpu.VMEM((HEADS, 1, tok), F32),
                pltpu.VMEM((HEADS, 1, tok), F32),
                pltpu.VMEM((n, q, d), BF16),
                dma((2,)),
                dma((n // 2, 3)),
                dma((n,)),
                dma((n // 2, 3)),
                dma((n,)),
            ],
            compiler_params=pltpu.CompilerParams(
                collective_id=0, has_side_effects=True, vmem_limit_bytes=60 * 1024 * 1024
            ),
        )(features, norm_gain.reshape(1, d), w_qkv, w_out, counts, query_index, owner)

    in_specs = (
        P(("scene", "frame"), None),
        P(),
        P(),
        P(),
        P("scene"),
        P(("scene", "frame"), None),
        P("scene"),
    )
    out_specs = (P(("scene", "frame"), None), P(("scene", "frame"), None, None, None))
    return jax.shard_map(
        per_device, mesh=mesh, in_specs=in_specs, out_specs=out_specs, check_vma=False
    )
```

```python
import functools

import jax
import jax.numpy as jnp
from jax import lax
from jax.experimental import pallas as pl
from jax.experimental.pallas import tpu as pltpu
from jax.sharding import PartitionSpec as P

HEADS = 16
MESH = pl.DeviceIdType.MESH
F32 = jnp.float32
BF16 = jnp.bfloat16
NT = (((1,), (1,)), ((), ()))
GROUP = 8


def kernel(
    n,
    f_ref, gain_ref, wqkv_hbm, wo_hbm, counts_ref, index_ref, owner_ref,
    mixed_ref, corr_ref,
    slots, w, wo, wvt, nrm, qt, kb, vt, acc, top, total, rows,
    wsem, send, recv, rsend, rrecv,
):
    tok, d = f_ref.shape
    hd = d // HEADS
    length = n // 2
    me = lax.axis_index("frame")
    a, b = me // 2, me % 2
    across = a * 2 + (1 - b)
    has_left, has_right = a > 0, a < length - 1

    copies = [
        pltpu.make_async_copy(wqkv_hbm, w, wsem.at[0]),
        pltpu.make_async_copy(wo_hbm, wo, wsem.at[1]),
    ]
    for c in copies:
        c.start()

    barrier = pltpu.get_barrier_semaphore()

    def greet(target):
        pl.semaphore_signal(barrier, inc=1, device_id={"frame": target}, device_id_type=MESH)

    pl.when(has_left)(lambda: greet(me - 2))
    pl.when(has_right)(lambda: greet(me + 2))
    greet(across)
    pl.semaphore_wait(
        barrier, 1 + jnp.where(has_left, 1, 0) + jnp.where(has_right, 1, 0)
    )

    def hop(buf, ssem, rsem, src, way, target, source=None):
        return pltpu.make_async_remote_copy(
            src_ref=buf.at[src] if source is None else source,
            dst_ref=buf.at[src],
            send_sem=ssem.at[src // 2, way],
            recv_sem=rsem.at[src],
            device_id={"frame": target},
            device_id_type=MESH,
        )

    def push(buf, ssem, rsem, src, go_right, go_left, source=None):
        pl.when(go_right)(lambda: hop(buf, ssem, rsem, src, 0, me + 2, source).start())
        pl.when(go_left)(lambda: hop(buf, ssem, rsem, src, 1, me - 2, source).start())
        hop(buf, ssem, rsem, src, 2, across, source).start()

    def landed(buf, ssem, rsem, src):
        hop(buf, ssem, rsem, src, 2, across).wait_recv()

    def relay(buf, ssem, rsem, dist):
        @pl.when(a - dist >= 0)
        def _():
            src = me - 2 * dist
            landed(buf, ssem, rsem, src)
            push(buf, ssem, rsem, src, has_right, False)

        @pl.when(a + dist <= length - 1)
        def _():
            src = me + 2 * dist
            landed(buf, ssem, rsem, src)
            push(buf, ssem, rsem, src, False, has_left)

    def drain(buf, ssem, rsem, source=None):
        hop(buf, ssem, rsem, me, 2, across, source).wait_send()
        pl.when(has_right)(lambda: hop(buf, ssem, rsem, me, 0, me + 2, source).wait_send())
        pl.when(has_left)(lambda: hop(buf, ssem, rsem, me, 1, me - 2, source).wait_send())

        @pl.loop(1, length)
        def _(dist):
            @pl.when(a - dist >= 0)
            def _():
                src = me - 2 * dist
                hop(buf, ssem, rsem, src, 2, across).wait_send()
                pl.when(has_right)(lambda: hop(buf, ssem, rsem, src, 0, me + 2).wait_send())

            @pl.when(a + dist <= length - 1)
            def _():
                src = me + 2 * dist
                hop(buf, ssem, rsem, src, 2, across).wait_send()
                pl.when(has_left)(lambda: hop(buf, ssem, rsem, src, 1, me - 2).wait_send())

    push(slots, send, recv, me, has_right, has_left, f_ref)

    near = jnp.minimum(a, length - 1 - a)

    def place(k):
        dist = jnp.where(k <= 2 * near, (k + 1) // 2, k - near)
        left = jnp.where(k <= 2 * near, k % 2 == 1, a >= length - 1 - a)
        return jnp.where(left, a - dist, a + dist)

    def normalize(load):
        step = 32

        @pl.loop(0, tok // step, unroll=2)
        def _(i):
            at = pl.ds(pl.multiple_of(i * step, step), step)
            x = load(at).astype(F32)
            mean = jnp.mean(x, axis=-1, keepdims=True)
            c = x - mean
            var = jnp.mean(c * c, axis=-1, keepdims=True)
            nrm[at, :] = (c * lax.rsqrt(var + 1e-05) * gain_ref[...]).astype(BF16)

    def attend():
        tile = 256
        for c in range(d // tile):
            kb[:, c * tile : (c + 1) * tile] = jnp.dot(
                nrm[...], w[:, d + c * tile : d + (c + 1) * tile], preferred_element_type=F32
            ).astype(BF16)
        for c in range(d // tile):
            vt[c * tile : (c + 1) * tile, :] = lax.dot_general(
                wvt[c * tile : (c + 1) * tile, :], nrm[...], NT, preferred_element_type=F32
            ).astype(BF16)

        @pl.loop(0, HEADS // GROUP)
        def _(g):
            hs = [g * GROUP + j for j in range(GROUP)]
            ss, ps, fades = [], [], []
            for j in range(GROUP):
                cols = pl.ds(pl.multiple_of((g * GROUP + j // 2 * 2) * hd, 2 * hd), 2 * hd)
                ss.append(jnp.dot(kb[:, cols], qt[hs[j]], preferred_element_type=F32))
            for j in range(GROUP):
                h, s = hs[j], ss[j]
                old = top[h]
                new = jnp.maximum(old, jnp.max(s, axis=0, keepdims=True))
                fade = jnp.exp(old - new)
                p = jnp.exp(s - new)
                top[h] = new
                total[h] = total[h] * fade + jnp.sum(p, axis=0, keepdims=True)
                fades.append(fade)
                ps.append(p.astype(BF16))
            for j in range(GROUP):
                at = pl.ds(pl.multiple_of(hs[j] * hd, hd), hd)
                acc[at, :] = acc[at, :] * fades[j] + jnp.dot(
                    vt[at, :], ps[j], preferred_element_type=F32
                )

    normalize(lambda at: f_ref[at, :])
    copies[0].wait()
    pair = 2 * hd
    upper = lax.broadcasted_iota(jnp.int32, (pair, tok), 0) < hd
    for c in range(HEADS // 2):
        q = jnp.dot(nrm[...], w[:, c * pair : (c + 1) * pair], preferred_element_type=F32)
        q = jnp.transpose(q * (1.0 / hd**0.5))
        qt[2 * c] = jnp.where(upper, q, 0.0).astype(BF16)
        qt[2 * c + 1] = jnp.where(upper, 0.0, q).astype(BF16)
    for c in range(d // 128):
        part = w[:, 2 * d + c * 128 : 2 * d + (c + 1) * 128].astype(F32)
        wvt[c * 128 : (c + 1) * 128, :] = jnp.transpose(part).astype(BF16)
    top[...] = jnp.full(top.shape, -1e30, F32)
    total[...] = jnp.zeros_like(total)
    acc[...] = jnp.zeros_like(acc)

    @pl.loop(0, n)
    def _(t):
        odd = t % 2 == 1
        by_line = jnp.logical_and(odd, t < n - 1)

        @pl.when(by_line)
        def _():
            relay(slots, send, recv, (t + 1) // 2)

        near_k = jnp.where(by_line, (t + 1) // 2, jnp.where(odd, length - 1, t // 2 - 1))
        src = jnp.where(
            t == 0, me, place(jnp.maximum(near_k, 0)) * 2 + jnp.where(by_line, b, 1 - b)
        )

        @pl.when(jnp.logical_and(t > 0, jnp.logical_not(by_line)))
        def _():
            landed(slots, send, recv, src)

        @pl.when(t > 0)
        def _():
            normalize(lambda at: slots[src, at, :])

        attend()

    tile = 256
    per = tile // hd
    for c in range(d // tile):
        o = jnp.concatenate(
            [
                acc[h * hd : (h + 1) * hd, :] / total[h]
                for h in range(c * per, (c + 1) * per)
            ],
            axis=0,
        )
        nrm[:, c * tile : (c + 1) * tile] = jnp.transpose(o).astype(BF16)
    copies[1].wait()
    for c in range(d // tile):
        cols = slice(c * tile, (c + 1) * tile)
        mixed_ref[:, cols] = (
            f_ref[:, cols].astype(F32)
            + jnp.dot(nrm[...], wo[:, cols], preferred_element_type=F32)
        ).astype(BF16)

    q = index_ref.shape[1]
    at = lax.broadcasted_iota(jnp.int32, (tok, q), 0)
    slot = lax.broadcasted_iota(jnp.int32, (tok, q), 1)
    chosen = jnp.logical_and(at == index_ref[...], slot < counts_ref[me])
    chosen = jnp.transpose(jnp.where(chosen, 1.0, 0.0).astype(F32)).astype(BF16)
    rows[me] = jnp.dot(chosen, mixed_ref[...], preferred_element_type=F32).astype(BF16)
    push(rows, rsend, rrecv, me, has_right, has_left)

    @pl.loop(1, length)
    def _(dist):
        relay(rows, rsend, rrecv, dist)

    @pl.loop(0, length)
    def _(k):
        landed(rows, rsend, rrecv, place(k) * 2 + 1 - b)

    scale = 1.0 / d**0.5
    for f0 in range(0, n, 8):
        fn = min(8, n - f0)
        block = rows[f0 : f0 + fn].reshape(fn * q, d)
        got = lax.dot_general(block, mixed_ref[...], NT, preferred_element_type=F32)
        for f in range(fn):
            factor = jnp.where(owner_ref[f0 + f] == me, scale, 0.0).astype(F32)
            corr_ref[0, f0 + f] = got[f * q : (f + 1) * q, :] * factor

    drain(slots, send, recv, f_ref)
    drain(rows, rsend, rrecv)


def solution(mesh):
    n = mesh.shape["frame"]

    def per_device(features, norm_gain, w_qkv, w_out, counts, query_index, owner):
        tok, d = features.shape
        q = query_index.shape[1]
        hd = d // HEADS
        vmem = pl.BlockSpec(memory_space=pltpu.VMEM)
        smem = pl.BlockSpec(memory_space=pltpu.SMEM)
        hbm = pl.BlockSpec(memory_space=pl.ANY)
        dma = pltpu.SemaphoreType.DMA
        return pl.pallas_call(
            functools.partial(kernel, n),
            out_shape=(
                jax.ShapeDtypeStruct((tok, d), BF16),
                jax.ShapeDtypeStruct((1, n, q, tok), F32),
            ),
            in_specs=[vmem, vmem, hbm, hbm, smem, vmem, smem],
            out_specs=(vmem, vmem),
            scratch_shapes=[
                pltpu.VMEM((n, tok, d), BF16),
                pltpu.VMEM((d, 3 * d), BF16),
                pltpu.VMEM((d, d), BF16),
                pltpu.VMEM((d, d), BF16),
                pltpu.VMEM((tok, d), BF16),
                pltpu.VMEM((HEADS, 2 * hd, tok), BF16),
                pltpu.VMEM((tok, d), BF16),
                pltpu.VMEM((d, tok), BF16),
                pltpu.VMEM((d, tok), F32),
                pltpu.VMEM((HEADS, 1, tok), F32),
                pltpu.VMEM((HEADS, 1, tok), F32),
                pltpu.VMEM((n, q, d), BF16),
                dma((2,)),
                dma((n // 2, 3)),
                dma((n,)),
                dma((n // 2, 3)),
                dma((n,)),
            ],
            compiler_params=pltpu.CompilerParams(
                collective_id=0, has_side_effects=True, vmem_limit_bytes=60 * 1024 * 1024
            ),
        )(features, norm_gain.reshape(1, d), w_qkv, w_out, counts, query_index, owner)

    in_specs = (
        P(("scene", "frame"), None),
        P(),
        P(),
        P(),
        P("scene"),
        P(("scene", "frame"), None),
        P("scene"),
    )
    out_specs = (P(("scene", "frame"), None), P(("scene", "frame"), None, None, None))
    return jax.shard_map(
        per_device, mesh=mesh, in_specs=in_specs, out_specs=out_specs, check_vma=False
    )
```
